32 devices in a mesh: pipe: 4 (over x, core), tensor: 2 (over y), dp: 4 (over z).
Axes of the slice: x: 2, y: 2, z: 4, core: 2. Of those that a mesh axis runs over, the one named last changes fastest.
Arguments:
- inputs: bfloat16 [2, 256, 4096], P(None, 'dp'), may hold values from -6 to 6
- layer_gain: float32 [4, 4096], P('pipe'), may hold values from 0.5 to 1.5
- up_weight: bfloat16 [4, 4096, 14336], P('pipe', 'dp', 'tensor'), may hold values from -0.09375 to 0.09375
- down_weight: bfloat16 [4, 14336, 4096], P('pipe', 'tensor', 'dp'), may hold values from -0.046875 to 0.046875
- final_gain: float32 [4096], replicated, may hold values from 0.5 to 1.5
- value_head: bfloat16 [4096], replicated, may hold values from -6 to 6
- q_head: bfloat16 [4096, 65536], P(None, ('pipe', 'tensor', 'dp')), may hold values from -620 to 620
- target_head: bfloat16 [4096, 65536], P(None, ('pipe', 'tensor', 'dp')), may hold values from -18 to 18
- actions: int32 [2, 256], replicated, may hold values from 0 to 65535
- rewards: int32 [2, 256], replicated, may hold values from -2 to 2
- done: int32 [2, 256], replicated, may hold values 0 or 1
- order: int32 [2], replicated, may hold values from 0 to 1, each once
Outputs:
- state_values: float32 [2, 256], replicated
- advantages: float32 [2, 256], replicated
- td_errors: float32 [2, 256], replicated
- value_loss: float32 [], replicated
- q_loss: float32 [], replicated
- lse_grad: bfloat16 [4096, 65536], P(None, ('pipe', 'tensor', 'dp'))
The draws below stay inside these ranges and needn't reach their ends.
Inputs may be any that keep to these rules, and one draw needn't show every extreme that they name: `order`: each micro-batch once.
All inputs are finite; a program needn't handle non-finite values.
Results may differ from the reference program's by a relative error of at most 0.04.
Values may be sent and summed in bfloat16 or wider, within the bound.
No kernel may reach another device: no remote copies, remote signals or barrier semaphores. Data moves between devices by JAX's collectives and lax.ppermute only.
A program may use at most 256 MiB of HBM per device.

```python
import jax
import jax.numpy as jnp
from jax import lax

D = 4096
FF = 14336
VQ = 65536
MB = 2
TOK_MB = 64
TOKS = 256
N_PIPE = 4


def draw_q_head(key, part):
    first = jax.random.fold_in(jax.random.fold_in(key, 17), 0)
    return jnp.clip(jax.random.normal(first, (D, VQ), jnp.float32) * 3.0, -18.0, 18.0).astype(jnp.bfloat16)


def touch_ends(drawn, own_key, low, high):
    extent = drawn.shape
    spot = [jax.random.randint(jax.random.fold_in(own_key, axis), (), 0, extent[axis]) for axis in range(len(extent))]
    drawn = drawn.at[tuple(spot)].set(low)
    longest = extent.index(max(extent))
    spot[longest] = (spot[longest] + 1) % extent[longest]
    return drawn.at[tuple(spot)].set(high)


def level_of(rng, extent, shards, low, largest):
    def one(position, shards_of):
        draws = jax.random.uniform(jax.random.fold_in(jax.random.fold_in(rng, 6), position), (shards_of,), jnp.float32, low / len(shards), largest / len(shards))
        return jnp.repeat(jnp.exp(draws), extent[position] // shards_of).reshape((-1,) + (1,) * (len(extent) - position - 1))

    level = one(*shards[0])
    for cut in shards[1:]:
        level = level * one(*cut)
    return level


def normal_values(key, dims, scale, reach, cuts=(), dtype=jnp.bfloat16):
    values = scale * jax.random.normal(key, dims, jnp.float32)
    if cuts:
        values = values * level_of(key, dims, cuts, -0.22, 0.18)
    return jnp.clip(values, -reach, reach).astype(dtype)


def setup_inputs(seed: int = 0) -> dict:
    key_list = jax.random.split(jax.random.key(seed), 13)
    return {
        "inputs": normal_values(key_list[0], (MB, TOKS, D), 1.0, 6.0, ((1, 4),)),
        "layer_gain": jnp.clip(1.0 + 0.1 * jax.random.normal(key_list[1], (N_PIPE, D), jnp.float32), 0.5, 1.5),
        "up_weight": normal_values(key_list[2], (N_PIPE, D, FF), D ** -0.5, 0.09375, ((0, 4), (1, 4), (2, 2))),
        "down_weight": normal_values(key_list[3], (N_PIPE, FF, D), FF ** -0.5, 0.046875, ((0, 4), (1, 2), (2, 4))),
        "final_gain": jnp.clip(1.0 + 0.1 * jax.random.normal(key_list[4], (D,), jnp.float32), 0.5, 1.5),
        "value_head": normal_values(key_list[5], (D,), 1.0, 6.0),
        "q_head": draw_q_head(jax.random.fold_in(key_list[12], 71), 0),
        "target_head": normal_values(key_list[7], (D, VQ), 3.0, 18.0, ((1, 32),)),
        "actions": touch_ends(jax.random.randint(key_list[8], (MB, TOKS), 0, VQ), jax.random.fold_in(key_list[8], 1), 0, VQ - 1).astype(jnp.int32),
        "rewards": touch_ends(jax.random.randint(key_list[9], (MB, TOKS), -2, 3), jax.random.fold_in(key_list[9], 1), -2, 2).astype(jnp.int32),
        "done": touch_ends((jax.random.randint(key_list[10], (MB, TOKS), 0, 8) < 1).astype(jnp.int32), jax.random.fold_in(key_list[10], 1), 0, 1),
        "order": jax.random.permutation(key_list[11], MB).astype(jnp.int32),
    }


EPS = 1e-05
GAMMA = 0.99
TAU = 0.7
ALPHA = 0.5

def normed(values, gain):
    wide = values.astype(jnp.float32)
    factor = lax.rsqrt(lax.optimization_barrier(jnp.mean(wide * wide, axis=-1, keepdims=True)) + EPS)
    return wide * factor * gain.astype(jnp.float32)

def block(states, gain, w_up, w_down):
    normal = normed(states, gain).astype(jnp.bfloat16)
    upper = jnp.dot(normal, w_up, preferred_element_type=jnp.float32)
    hidden = jax.nn.silu(upper).astype(jnp.bfloat16)
    return (states.astype(jnp.float32) + jnp.dot(hidden, w_down, preferred_element_type=jnp.float32)).astype(jnp.bfloat16)

def reference(inputs, layer_gain, up_weight, down_weight, final_gain, value_head, q_head, target_head, actions, rewards, done, order):
    chosen = jnp.take(inputs, order, axis=0)
    states = chosen.reshape(MB * TOKS, D)
    for section in range(N_PIPE):
        states = block(states, layer_gain[section], up_weight[section], down_weight[section])
    final = normed(states, final_gain).astype(jnp.bfloat16)
    action = jnp.take(actions, order, axis=0).reshape(-1).astype(jnp.int32)
    reward = jnp.take(rewards, order, axis=0).reshape(-1).astype(jnp.float32)
    finished = jnp.take(done, order, axis=0).reshape(-1).astype(jnp.float32)
    factor = D ** (-0.5)
    values = jnp.dot(final, value_head, preferred_element_type=jnp.float32) * factor
    logits = jnp.dot(final, q_head, preferred_element_type=jnp.float32) * factor
    top = lax.optimization_barrier(jnp.max(logits, axis=-1))
    total = lax.optimization_barrier(jnp.sum(jnp.exp(logits - top[:, None]), axis=-1))
    lse = top + jnp.log(total)
    column = lax.broadcasted_iota(jnp.int32, (1, VQ), 1)
    onehot = (action[:, None] == column).astype(jnp.float32)
    taken = lax.optimization_barrier(jnp.sum(logits * onehot, axis=-1))
    target_cols = jnp.take(target_head, action, axis=1)
    target_taken = lax.optimization_barrier(jnp.sum(final.astype(jnp.float32) * target_cols.T.astype(jnp.float32), axis=-1)) * factor
    windows = values.reshape(-1, TOK_MB)
    following = jnp.concatenate([windows[:, 1:], jnp.zeros((windows.shape[0], 1), jnp.float32)], axis=1).reshape(-1)
    bootstrap = 0.5 * reward + GAMMA * (1.0 - finished) * following
    td_value = taken - bootstrap
    advantage = target_taken - values
    weight = jnp.where(advantage < 0, 1.0 - TAU, TAU)
    value_loss = jnp.mean(weight * advantage * advantage)
    q_loss = jnp.mean(td_value * td_value + ALPHA * (lse - taken))
    probs = jnp.exp(logits - lse[:, None]).astype(jnp.bfloat16)
    scale = VQ * factor / (MB * TOKS)
    summed = lax.dot_general(final, probs, (((0,), (0,)), ((), ())), preferred_element_type=jnp.float32)
    lse_grad = (summed * scale).astype(jnp.bfloat16)
    shape = (MB, TOKS)
    return (values.reshape(shape), advantage.reshape(shape), td_value.reshape(shape), value_loss, q_loss, lse_grad)
```

```python
import jax
import jax.numpy as jnp
from jax import lax
from jax.sharding import PartitionSpec as P

VQ = 65536


EPS = 1e-05
GAMMA = 0.99
TAU = 0.7
ALPHA = 0.5

AXES = ("pipe", "tensor", "dp")


def send(block, pairs):
    _, tensors, dps = (lax.axis_size(a) for a in AXES)

    def flat(c):
        return (c[0] * tensors + c[1]) * dps + c[2]

    return lax.ppermute(block, AXES, [(flat(a), flat(b)) for a, b in pairs])


def along_dp(block, pipe, moves):
    pipes = [p for p in range(lax.axis_size("pipe")) if p % 2 == pipe % 2]
    rows = range(lax.axis_size("tensor"))
    pairs = [((p, t, a), (p, t, b)) for p in pipes for t in rows for a, b in moves]
    return send(block, pairs)


def over_cells(block, hops, across=False):
    tensors, dps = lax.axis_size("tensor"), lax.axis_size("dp")
    cells = [(t, d) for t in range(tensors) for d in range(dps)]
    flip = 1 if across else 0
    return send(block, [((a, t, d), (b, t ^ flip, d)) for a, b in hops for t, d in cells])


OUTER = ((0, 1), (3, 2))
OUTWARD = ((1, 0), (2, 3))
MIDDLE = ((1, 2), (2, 1))
SWAP = ((0, 1), (1, 0), (2, 3), (3, 2))
SKIP = ((0, 2), (2, 0), (1, 3), (3, 1))
MIRROR = ((0, 3), (3, 0), (1, 2), (2, 1))


def gathered(own, pipe):
    rank = lax.axis_index("dp")
    inner = (rank == 1) | (rank == 2)
    next1 = along_dp(own, pipe, SWAP)
    middle = along_dp(own, pipe, MIDDLE)
    next2_inner = along_dp(next1, pipe, MIDDLE)
    next2_outer = along_dp(middle, pipe, OUTWARD)
    next3_outer = along_dp(next2_inner, pipe, OUTWARD)
    next2 = jnp.where(inner, next2_inner, next2_outer)
    next3 = jnp.where(inner, middle, next3_outer)
    return own, next1, next2, next3


def hidden_layer(states, gain, w_up, w_down, pipe):
    rank = lax.axis_index("dp")
    size = lax.axis_size("dp")
    rows, width = states.shape
    block = w_up.shape[1] // size
    wide = states.astype(jnp.float32)
    scaled = (wide * gain).astype(jnp.bfloat16)
    squares = jnp.sum(wide * wide, axis=1)
    squares = squares + along_dp(squares, pipe, SWAP)
    squares = squares + along_dp(squares, pipe, SKIP)
    factor = lax.rsqrt(squares / (width * size) + EPS)[:, None]

    def part(flip):
        columns = lax.dynamic_slice_in_dim(w_up, (rank ^ flip) * block, block, 1)
        return jnp.dot(scaled, columns, preferred_element_type=jnp.float32)

    def lower(values):
        return values.astype(jnp.bfloat16)

    def add(values, other):
        return values + other.astype(jnp.float32)

    part3 = part(3)
    far = along_dp(lower(part3), pipe, OUTER)
    sum2 = lower(add(part(2), far))
    outer2 = along_dp(sum2, pipe, OUTER)
    middle2 = along_dp(sum2, pipe, MIDDLE)
    sum1 = lower(add(part(1), middle2))
    near = along_dp(sum1, pipe, SWAP)
    cross = along_dp(lower(add(part3, outer2)), pipe, MIDDLE)
    upper = add(add(part(0), near), cross) * factor
    own = lower(jax.nn.silu(upper))
    total = jnp.zeros((rows, width), jnp.float32)
    for flip, piece in enumerate(gathered(own, pipe)):
        weights = lax.dynamic_slice_in_dim(w_down, (rank ^ flip) * block, block, 0)
        total = total + jnp.dot(piece, weights, preferred_element_type=jnp.float32)
    return total


def first_states(chosen):
    rank = lax.axis_index("dp")
    size = lax.axis_size("dp")
    window, width = chosen.shape
    share = width // size
    states = jnp.zeros((size, window, share), chosen.dtype)
    for flip, moves in enumerate((None, SWAP, SKIP, MIRROR)):
        piece = lax.dynamic_slice_in_dim(chosen, (rank ^ flip) * share, share, 1)
        if flip:
            piece = along_dp(piece, 0, moves)
        states = lax.dynamic_update_slice_in_dim(states, piece[None], rank ^ flip, 0)
    return states.reshape(size * window, share)


def handed_on(states, total, hops):
    tensors = lax.axis_size("tensor")
    if tensors == 2:
        mine = lax.axis_index("tensor") == 0
        base = jnp.where(mine, states.astype(jnp.float32), 0.0)
        part = (base + total).astype(jnp.bfloat16)
        straight = over_cells(part, hops)
        across = over_cells(part, hops, across=True)
        return (straight.astype(jnp.float32) + across.astype(jnp.float32)).astype(jnp.bfloat16)
    whole = (states.astype(jnp.float32) + lax.psum(total, "tensor")).astype(jnp.bfloat16)
    return over_cells(whole, hops)


def next_hops(pipe, sections):
    if pipe % 2 == 0:
        return [(p, p + 1) for p in range(0, sections - 1, 2)]
    return [(pipe, pipe + 1)]


def final_states(states, total):
    sections = lax.axis_size("pipe")
    rank = lax.axis_index("dp")
    pipe = lax.axis_index("pipe")
    last = sections - 1
    done = handed_on(states, total, [(last, last - 1)])
    for target in range(0, last - 1, 2):
        moved = over_cells(done, [(last - 1, target)])
        done = jnp.where(pipe == target, moved, done)
    rows, share = done.shape
    size = lax.axis_size("dp")
    whole = jnp.zeros((rows, size * share), done.dtype)
    for flip, piece in enumerate(gathered(done, 0)):
        whole = lax.dynamic_update_slice_in_dim(whole, piece, (rank ^ flip) * share, 1)
    twin = over_cells(whole, [(p, p + 1) for p in range(0, sections - 1, 2)])
    return jnp.where(pipe % 2 == 0, whole, twin)


def merged_stats(stats, combine):
    pipes, tensors, dps = (lax.axis_size(a) for a in AXES)

    def everywhere(value, route):
        cells = [(p, t, d) for p in range(pipes) for t in range(tensors) for d in range(dps)]
        return send(value, [(c, route(*c)) for c in cells])

    for axis, size in enumerate((pipes, tensors, dps)):
        bit = 1
        while bit < size:
            flips = [bit if i == axis else 0 for i in range(3)]
            other = everywhere(stats, lambda *c, f=flips: tuple(i ^ j for i, j in zip(c, f)))
            stats = combine(stats, other)
            bit *= 2
    return stats


def combine_stats(first, second):
    top = jnp.maximum(first[0], second[0])
    total = first[1] * jnp.exp(first[0] - top) + second[1] * jnp.exp(second[0] - top)
    return jnp.stack([top, total, first[2] + second[2], first[3] + second[3]])


def local(
    inputs,
    layer_gain,
    up_weight,
    down_weight,
    final_gain,
    value_head,
    q_head,
    target_head,
    actions,
    rewards,
    done,
    order,
):
    sections = lax.axis_size("pipe")
    micro = inputs.shape[0]
    window = inputs.shape[1]
    width_model = inputs.shape[2]
    share = width_model // lax.axis_size("dp")
    w_up, w_down = up_weight[0], down_weight[0]
    gain = lax.dynamic_slice_in_dim(layer_gain[0], lax.axis_index("dp") * share, share, 0)

    columns_here = q_head.shape[1]
    offset = lax.axis_index(AXES) * columns_here
    action = jnp.take(actions, order, axis=0).reshape(-1)
    reward = jnp.take(rewards, order, axis=0).reshape(-1).astype(jnp.float32)
    finished = jnp.take(done, order, axis=0).reshape(-1).astype(jnp.float32)
    hit = action[:, None] == offset + lax.broadcasted_iota(jnp.int32, (1, columns_here), 1)
    target_rows = lax.dot_general(
        hit.astype(jnp.bfloat16),
        target_head,
        (((1,), (1,)), ((), ())),
        preferred_element_type=jnp.float32,
    ).astype(jnp.bfloat16)
    target_rows = lax.optimization_barrier(target_rows)

    chosen = jnp.take(inputs, order, axis=0)
    streams = [first_states(chosen[m]) for m in range(micro)]
    for pipe in range(sections):
        for m in range(micro):
            total = hidden_layer(streams[m], gain, w_up, w_down, pipe)
            if pipe < sections - 1:
                streams[m] = handed_on(streams[m], total, next_hops(pipe, sections))
            else:
                streams[m] = final_states(streams[m], total)
    raw = jnp.concatenate(streams, axis=0)

    wide = raw.astype(jnp.float32)
    scale_row = lax.rsqrt(jnp.mean(wide * wide, axis=-1, keepdims=True) + EPS)
    flat = (wide * scale_row * final_gain).astype(jnp.bfloat16)
    count = flat.shape[0]
    factor = width_model ** (-0.5)
    values = jnp.dot(flat, value_head, preferred_element_type=jnp.float32) * factor
    logits = jnp.dot(flat, q_head, preferred_element_type=jnp.float32) * factor
    local_top = jnp.max(logits, axis=-1)
    local_total = jnp.sum(jnp.exp(logits - local_top[:, None]), axis=-1)
    taken_part = jnp.sum(jnp.where(hit, logits, 0.0), axis=-1)
    target_part = (
        jnp.sum(flat.astype(jnp.float32) * target_rows.astype(jnp.float32), axis=-1) * factor
    )
    stats = merged_stats(
        jnp.stack([local_top, local_total, taken_part, target_part]), combine_stats
    )
    highest, summed, taken, target_taken = stats[0], stats[1], stats[2], stats[3]
    lse = highest + jnp.log(summed)
    windows = values.reshape(-1, window)
    following = jnp.concatenate(
        [windows[:, 1:], jnp.zeros((windows.shape[0], 1), jnp.float32)], axis=1
    ).reshape(-1)
    bootstrap = 0.5 * reward + GAMMA * (1.0 - finished) * following
    td_value = taken - bootstrap
    advantage = target_taken - values
    weight = jnp.where(advantage < 0, 1.0 - TAU, TAU)
    value_loss = jnp.mean(weight * advantage * advantage)
    q_loss = jnp.mean(td_value * td_value + ALPHA * (lse - taken))
    probs = jnp.exp(logits - lse[:, None]).astype(jnp.bfloat16)
    scale = VQ * factor / count
    gathered_sum = lax.dot_general(
        flat, probs, (((0,), (0,)), ((), ())), preferred_element_type=jnp.float32
    )
    lse_grad = (gathered_sum * scale).astype(jnp.bfloat16)
    shape = (micro, count // micro)
    return (
        values.reshape(shape),
        advantage.reshape(shape),
        td_value.reshape(shape),
        value_loss,
        q_loss,
        lse_grad,
    )


def solution(mesh):
    in_specs = (
        P(None, "dp", None),
        P("pipe", None),
        P("pipe", "dp", "tensor"),
        P("pipe", "tensor", "dp"),
        P(),
        P(),
        P(None, ("pipe", "tensor", "dp")),
        P(None, ("pipe", "tensor", "dp")),
        P(),
        P(),
        P(),
        P(),
    )
    out_specs = (P(), P(), P(), P(), P(), P(None, ("pipe", "tensor", "dp")))
    return jax.shard_map(local, mesh=mesh, in_specs=in_specs, out_specs=out_specs, check_vma=False)
```

```python
import jax
import jax.numpy as jnp
from jax import lax
from jax.sharding import PartitionSpec as P

VQ = 65536


EPS = 1e-05
GAMMA = 0.99
TAU = 0.7
ALPHA = 0.5

AXES = ("pipe", "tensor", "dp")


def send(block, pairs):
    _, tensors, dps = (lax.axis_size(a) for a in AXES)

    def flat(c):
        return (c[0] * tensors + c[1]) * dps + c[2]

    return lax.ppermute(block, AXES, [(flat(a), flat(b)) for a, b in pairs])


def everywhere(block, route):
    pipes, tensors, dps = (range(lax.axis_size(a)) for a in AXES)
    cells = [(p, t, d) for p in pipes for t in tensors for d in dps]
    return send(block, [(c, route(*c)) for c in cells])


def along_dp(block, moves):
    pipes, tensors = range(lax.axis_size("pipe")), range(lax.axis_size("tensor"))
    pairs = [((p, t, a), (p, t, b)) for p in pipes for t in tensors for a, b in moves]
    return send(block, pairs)


SWAP = ((0, 1), (1, 0), (2, 3), (3, 2))
SKIP = ((0, 2), (2, 0), (1, 3), (3, 1))
MIRROR = ((0, 3), (3, 0), (1, 2), (2, 1))


def across_middle(block):
    return everywhere(
        block, lambda p, t, d: (p, t, 3 - d) if d in (1, 2) else (p ^ 1, t, d)
    )


def to_twin(block):
    return everywhere(block, lambda p, t, d: (p ^ 1, t, d))


def lower(values):
    return values.astype(jnp.bfloat16)


def add(values, other):
    return values + other.astype(jnp.float32)


def only(where, values):
    return jnp.where(where, values.astype(jnp.float32), 0.0)


def is_inner():
    rank = lax.axis_index("dp")
    return (rank == 1) | (rank == 2)


class Weights:
    def __init__(self, w_up, w_down, gain):
        self.gain, self.gain_got = gain, to_twin(gain)
        self.core = lax.axis_index("pipe") % 2
        self.half = w_up.shape[1] // 2
        self.block = self.half // lax.axis_size("dp")
        self.up, self.down = w_up, w_down
        there = (1 - self.core) * self.half
        self.up_got = to_twin(lax.dynamic_slice_in_dim(w_up, there, self.half, 1))
        self.down_got = to_twin(lax.dynamic_slice_in_dim(w_down, there, self.half, 0))

    def pick(self, mine, got, axis, section, flip):
        first = (lax.axis_index("dp") ^ flip) * self.block
        kept = lax.dynamic_slice_in_dim(mine, self.core * self.half + first, self.block, axis)
        moved = lax.dynamic_slice_in_dim(got, first, self.block, axis)
        return jnp.where(self.core == section % 2, kept, moved)

    def section_gain(self, section):
        return jnp.where(self.core == section % 2, self.gain, self.gain_got)

    def up_block(self, section, flip):
        return self.pick(self.up, self.up_got, 1, section, flip)

    def down_block(self, section, flip):
        return self.pick(self.down, self.down_got, 0, section, flip)


class Reduction:
    def __init__(self, states, weights, section):
        rows, width = states.shape
        wide = states.astype(jnp.float32)
        self.states = states
        self.section = section
        scaled = lower(wide * weights.section_gain(section))
        squares = jnp.sum(wide * wide, axis=1)
        self.squares = squares
        self.width = width * lax.axis_size("dp")

        def part(flip):
            block = weights.up_block(section, flip)
            return jnp.dot(scaled, block, preferred_element_type=jnp.float32)

        self.part = part
        self.part3 = part(3)


def both_ways(swapped, crossed, extra=None):
    if extra is None:
        swapped, crossed = lax.optimization_barrier((swapped, crossed))
        return lax.optimization_barrier((along_dp(swapped, SWAP), across_middle(crossed)))
    value, moves = extra
    swapped, crossed, value = lax.optimization_barrier((swapped, crossed, value))
    moved = along_dp(value, moves)
    outs = (along_dp(swapped, SWAP), across_middle(crossed), moved)
    return lax.optimization_barrier(outs)


def slot(own, reduction):
    inner = is_inner()
    y = reduction
    pieces = None
    if own is not None:
        near1, middle1 = both_ways(own, own)
    if own is None:
        got = along_dp(lower(y.part3), SWAP)
        squares = y.squares + along_dp(y.squares, SWAP)
    elif y is None:
        got, middle2 = both_ways(middle1, near1)
    else:
        got, middle2, other = both_ways(
            jnp.where(inner, middle1, lower(y.part3)), near1, (y.squares, SWAP)
        )
        squares = y.squares + other
    if y is None:
        got2 = along_dp(middle2, SWAP)
    else:
        part2 = y.part(2)
        crossed = lower(add(part2, got))
        swapped = lower(part2) if own is None else jnp.where(inner, middle2, lower(part2))
        got2, middle3, other = both_ways(swapped, crossed, (squares, SKIP))
        factor = lax.rsqrt((squares + other) / y.width + EPS)[:, None]
    if own is not None:
        pieces = (own, near1, jnp.where(inner, middle2, got), jnp.where(inner, middle1, got2))
    if y is None:
        return pieces, None
    last, cross = both_ways(
        lower(y.part(1) + only(inner, middle3)), lower(add(y.part3, got2))
    )
    upper = (add(y.part(0), last) + only(inner, cross)) * factor
    return pieces, lower(jax.nn.silu(upper))


def lowered(pieces, weights, section):
    total = None
    for flip, piece in enumerate(pieces):
        block = weights.down_block(section, flip)
        product = jnp.dot(piece, block, preferred_element_type=jnp.float32)
        total = product if total is None else total + product
    return total


def half_output(states, total):
    core = lax.axis_index("pipe") % 2
    half = states.shape[0] // 2

    def cut(values, index):
        return lax.dynamic_slice_in_dim(values, index * half, half, 0)

    both = add(cut(total, core), to_twin(lower(cut(total, 1 - core))))
    base = cut(states, core).astype(jnp.float32)
    if lax.axis_size("tensor") == 2:
        other = everywhere(lower(both), lambda p, t, d: (p, 1 - t, d))
        return lower(add(base + both, other))
    return lower(base + lax.psum(both, "tensor"))


def both_halves(half, axis=0):
    other = to_twin(half)
    first = lax.axis_index("pipe") % 2 == 0
    return jnp.concatenate(
        [jnp.where(first, half, other), jnp.where(first, other, half)], axis=axis
    )


def handed_on(states, total, section):
    half = half_output(states, total)
    if section % 2 == 1:
        sections = lax.axis_size("pipe")
        half = everywhere(half, lambda p, t, d: ((p + 2) % sections, t, d))
    return both_halves(half)


def first_states(chosen):
    rank = lax.axis_index("dp")
    size = lax.axis_size("dp")
    window, width = chosen.shape
    share = width // size
    states = jnp.zeros((size, window, share), chosen.dtype)
    for flip, moves in enumerate((None, SWAP, SKIP, MIRROR)):
        piece = lax.dynamic_slice_in_dim(chosen, (rank ^ flip) * share, share, 1)
        if flip:
            piece = along_dp(piece, moves)
        states = lax.dynamic_update_slice_in_dim(states, piece[None], rank ^ flip, 0)
    return states.reshape(size * window, share)


def final_states(states, total):
    sections = lax.axis_size("pipe")
    rank = lax.axis_index("dp")
    size = lax.axis_size("dp")
    pair = lax.axis_index("pipe") // 2
    half = half_output(states, total)
    last = sections // 2 - 1
    moved = half
    for turn in range(1, sections // 2):
        moved = everywhere(moved, lambda p, t, d: ((p + 2) % sections, t, d))
        half = jnp.where(pair == (last + turn) % (sections // 2), moved, half)
    pieces, _ = slot(half, None)
    rows, share = half.shape
    whole = jnp.zeros((rows, size * share), half.dtype)
    for flip, piece in enumerate(pieces):
        whole = lax.dynamic_update_slice_in_dim(whole, piece, (rank ^ flip) * share, 1)
    return both_halves(whole)


def merged_stats(stats, combine):
    pipes, tensors, dps = (lax.axis_size(a) for a in AXES)
    for axis, size in enumerate((pipes, tensors, dps)):
        bit = 1
        while bit < size:
            flips = [bit if i == axis else 0 for i in range(3)]
            other = everywhere(stats, lambda *c, f=flips: tuple(i ^ j for i, j in zip(c, f)))
            stats = combine(stats, other)
            bit *= 2
    return stats


def combine_stats(first, second):
    top = jnp.maximum(first[0], second[0])
    total = first[1] * jnp.exp(first[0] - top) + second[1] * jnp.exp(second[0] - top)
    return jnp.stack([top, total, first[2] + second[2], first[3] + second[3]])


def local(
    inputs,
    layer_gain,
    up_weight,
    down_weight,
    final_gain,
    value_head,
    q_head,
    target_head,
    actions,
    rewards,
    done,
    order,
):
    sections = lax.axis_size("pipe")
    micro = inputs.shape[0]
    window = inputs.shape[1]
    width_model = inputs.shape[2]
    share = width_model // lax.axis_size("dp")
    w_up, w_down = up_weight[0], down_weight[0]
    gain = lax.dynamic_slice_in_dim(layer_gain[0], lax.axis_index("dp") * share, share, 0)

    columns_here = q_head.shape[1]
    offset = lax.axis_index(AXES) * columns_here
    action = jnp.take(actions, order, axis=0).reshape(-1)
    reward = jnp.take(rewards, order, axis=0).reshape(-1).astype(jnp.float32)
    finished = jnp.take(done, order, axis=0).reshape(-1).astype(jnp.float32)
    hit = action[:, None] == offset + lax.broadcasted_iota(jnp.int32, (1, columns_here), 1)
    target_rows = lower(
        lax.dot_general(
            hit.astype(jnp.bfloat16),
            target_head,
            (((1,), (1,)), ((), ())),
            preferred_element_type=jnp.float32,
        )
    )

    weights = Weights(w_up, w_down, gain)
    chosen = jnp.take(inputs, order, axis=0)
    pending = [first_states(chosen[m]) for m in range(micro)]
    count = action.shape[0]
    pending[0], target_rows = lax.optimization_barrier((pending[0], target_rows))
    finals = []
    own = None
    holder = None
    for step in range(micro * sections + 1):
        stream, section = step % micro, step // micro
        reduction = None
        if step < micro * sections:
            reduction = Reduction(pending[stream], weights, section)
        pieces, fresh = slot(own, reduction)
        if own is not None:
            total = lowered(pieces, weights, holder.section)
            if holder.section < sections - 1:
                pending[(step - 1) % micro] = handed_on(holder.states, total, holder.section)
            else:
                finals.append(final_states(holder.states, total))
        own, holder = fresh, reduction
    raw = jnp.concatenate(finals, axis=0)

    wide = raw.astype(jnp.float32)
    scale_row = lax.rsqrt(jnp.mean(wide * wide, axis=-1, keepdims=True) + EPS)
    flat = (wide * scale_row * final_gain).astype(jnp.bfloat16)
    factor = width_model ** (-0.5)
    values = jnp.dot(flat, value_head, preferred_element_type=jnp.float32) * factor
    logits = jnp.dot(flat, q_head, preferred_element_type=jnp.float32) * factor
    local_top = jnp.max(logits, axis=-1)
    local_total = jnp.sum(jnp.exp(logits - local_top[:, None]), axis=-1)
    taken_part = jnp.sum(jnp.where(hit, logits, 0.0), axis=-1)
    target_part = (
        jnp.sum(flat.astype(jnp.float32) * target_rows.astype(jnp.float32), axis=-1) * factor
    )
    stats = merged_stats(
        jnp.stack([local_top, local_total, taken_part, target_part]), combine_stats
    )
    highest, summed, taken, target_taken = stats[0], stats[1], stats[2], stats[3]
    lse = highest + jnp.log(summed)
    windows = values.reshape(-1, window)
    following = jnp.concatenate(
        [windows[:, 1:], jnp.zeros((windows.shape[0], 1), jnp.float32)], axis=1
    ).reshape(-1)
    bootstrap = 0.5 * reward + GAMMA * (1.0 - finished) * following
    td_value = taken - bootstrap
    advantage = target_taken - values
    weight = jnp.where(advantage < 0, 1.0 - TAU, TAU)
    value_loss = jnp.mean(weight * advantage * advantage)
    q_loss = jnp.mean(td_value * td_value + ALPHA * (lse - taken))
    probs = jnp.exp(logits - lse[:, None]).astype(jnp.bfloat16)
    scale = VQ * factor / count
    gathered_sum = lax.dot_general(
        flat, probs, (((0,), (0,)), ((), ())), preferred_element_type=jnp.float32
    )
    lse_grad = (gathered_sum * scale).astype(jnp.bfloat16)
    shape = (micro, count // micro)
    return (
        values.reshape(shape),
        advantage.reshape(shape),
        td_value.reshape(shape),
        value_loss,
        q_loss,
        lse_grad,
    )


def solution(mesh):
    in_specs = (
        P(None, "dp", None),
        P("pipe", None),
        P("pipe", "dp", "tensor"),
        P("pipe", "tensor", "dp"),
        P(),
        P(),
        P(None, ("pipe", "tensor", "dp")),
        P(None, ("pipe", "tensor", "dp")),
        P(),
        P(),
        P(),
        P(),
    )
    out_specs = (P(), P(), P(), P(), P(), P(None, ("pipe", "tensor", "dp")))
    return jax.shard_map(local, mesh=mesh, in_specs=in_specs, out_specs=out_specs, check_vma=False)
```

```python
import jax
import jax.numpy as jnp
from jax import lax
from jax.sharding import PartitionSpec as P

VQ = 65536


EPS = 1e-05
GAMMA = 0.99
TAU = 0.7
ALPHA = 0.5

AXES = ("pipe", "tensor", "dp")


def send(block, pairs):
    _, tensors, dps = (lax.axis_size(a) for a in AXES)

    def flat(c):
        return (c[0] * tensors + c[1]) * dps + c[2]

    return lax.ppermute(block, AXES, [(flat(a), flat(b)) for a, b in pairs])


def everywhere(block, route):
    pipes, tensors, dps = (range(lax.axis_size(a)) for a in AXES)
    cells = [(p, t, d) for p in pipes for t in tensors for d in dps]
    return send(block, [(c, route(*c)) for c in cells])


def along_dp(block, moves):
    pipes, tensors = range(lax.axis_size("pipe")), range(lax.axis_size("tensor"))
    pairs = [((p, t, a), (p, t, b)) for p in pipes for t in tensors for a, b in moves]
    return send(block, pairs)


SWAP = ((0, 1), (1, 0), (2, 3), (3, 2))
SKIP = ((0, 2), (2, 0), (1, 3), (3, 1))
MIRROR = ((0, 3), (3, 0), (1, 2), (2, 1))


def across_middle(block):
    return everywhere(
        block, lambda p, t, d: (p, t, 3 - d) if d in (1, 2) else (p ^ 1, t, d)
    )


def to_twin(block):
    return everywhere(block, lambda p, t, d: (p ^ 1, t, d))


def lower(values):
    return values.astype(jnp.bfloat16)


def add(values, other):
    return values + other.astype(jnp.float32)


def only(where, values):
    return jnp.where(where, values.astype(jnp.float32), 0.0)


def is_inner():
    rank = lax.axis_index("dp")
    return (rank == 1) | (rank == 2)


class Weights:
    def __init__(self, w_up, w_down, gain):
        self.gain, self.gain_got = gain, to_twin(gain)
        self.core = lax.axis_index("pipe") % 2
        self.half = w_up.shape[1] // 2
        self.block = self.half // lax.axis_size("dp")
        self.mine = (w_up, w_down)
        self.got = ({}, {})
        self.ready = {}

    def swap(self, kind, flips, token=None):
        for flip in flips:
            sent = self.cut(kind, 1 - self.core, flip, token)
            self.got[kind][flip] = to_twin(sent)
        return sent

    def cut(self, kind, half, flip, token=None):
        rank = lax.axis_index("dp")
        if token is not None:
            rank, _ = lax.optimization_barrier((rank, token))
        first = half * self.half + (rank ^ flip) * self.block
        return lax.dynamic_slice_in_dim(self.mine[kind], first, self.block, 1 - kind)

    def section_gain(self, parity):
        return jnp.where(self.core == parity, self.gain, self.gain_got)

    def make(self, kind, parity, flips, moved):
        return tuple(
            jnp.where(self.core == parity, self.cut(kind, self.core, flip, block), block)
            for flip, block in zip(flips, moved)
        )

    def keep(self, kind, parity, flips, made):
        for flip, block in zip(flips, made):
            self.ready[kind, parity, flip] = block

    def work(self, kind, parity, flips):
        return (
            lambda: tuple(self.got[kind][f] for f in flips),
            lambda moved: self.make(kind, parity, flips, moved),
            lambda made: self.keep(kind, parity, flips, made),
        )

    def up_block(self, parity, flip):
        return self.ready[0, parity, flip]

    def down_block(self, parity, flip):
        return self.ready[1, parity, flip]


class Reduction:
    def __init__(self, states, weights, parity):
        width = states.shape[1]
        wide = states.astype(jnp.float32)
        self.states = states
        self.parity = parity
        scaled = lower(wide * weights.section_gain(parity))
        self.squares = jnp.sum(wide * wide, axis=1)
        self.width = width * lax.axis_size("dp")

        def part(flip):
            block = weights.up_block(parity, flip)
            return jnp.dot(scaled, block, preferred_element_type=jnp.float32)

        self.part = part
        self.part3 = part(3)


def together(moves, work=()):
    values = tuple(value for value, _ in moves)
    needs = tuple(need() for need, _, _ in work)
    values, needs = lax.optimization_barrier((values, needs))
    outs = tuple(move(value) for value, (_, move) in zip(values, moves))
    made = tuple(compute(need) for need, (_, compute, _) in zip(needs, work))
    outs, made = lax.optimization_barrier((outs, made))
    for result, (_, _, take) in zip(made, work):
        take(result)
    return outs


def swap_dp(block):
    return along_dp(block, SWAP)


def skip_dp(block):
    return along_dp(block, SKIP)


def slot(own, reduction, work=None):
    inner = is_inner()
    y = reduction
    pieces = None
    work = work or {}
    if own is not None:
        near1, middle1 = together(
            [(own, swap_dp), (own, across_middle)], work.get(1, ())
        )
    if own is None:
        got, other = together(
            [(lower(y.part3), swap_dp), (y.squares, swap_dp)], work.get(2, ())
        )
    elif y is None:
        got, middle2 = together(
            [(middle1, swap_dp), (near1, across_middle)], work.get(2, ())
        )
    else:
        swapped = jnp.where(inner, middle1, lower(y.part3))
        got, middle2, other = together(
            [(swapped, swap_dp), (near1, across_middle), (y.squares, swap_dp)], work.get(2, ())
        )
    if y is None:
        (got2,) = together([(middle2, swap_dp)], work.get(3, ()))
    else:
        squares = y.squares + other
        part2 = y.part(2)
        crossed = lower(add(part2, got))
        swapped = lower(part2) if own is None else jnp.where(inner, middle2, lower(part2))
        got2, middle3, other = together(
            [(swapped, swap_dp), (crossed, across_middle), (squares, skip_dp)], work.get(3, ())
        )
        factor = lax.rsqrt((squares + other) / y.width + EPS)[:, None]
    if own is not None:
        pieces = (own, near1, jnp.where(inner, middle2, got), jnp.where(inner, middle1, got2))
    if y is None:
        return pieces, None
    last, cross = together(
        [
            (lower(y.part(1) + only(inner, middle3)), swap_dp),
            (lower(add(y.part3, got2)), across_middle),
        ],
        work.get(4, ()),
    )
    upper = (add(y.part(0), last) + only(inner, cross)) * factor
    return pieces, lower(jax.nn.silu(upper))


def lowered(pieces, weights, parity):
    total = None
    for flip, piece in enumerate(pieces):
        block = weights.down_block(parity, flip)
        product = jnp.dot(piece, block, preferred_element_type=jnp.float32)
        total = product if total is None else total + product
    return total


def half_output(states, total):
    core = lax.axis_index("pipe") % 2
    half = states.shape[0] // 2

    def cut(values, index):
        return lax.dynamic_slice_in_dim(values, index * half, half, 0)

    both = add(cut(total, core), to_twin(lower(cut(total, 1 - core))))
    base = cut(states, core).astype(jnp.float32)
    if lax.axis_size("tensor") == 2:
        other = everywhere(lower(both), lambda p, t, d: (p, 1 - t, d))
        return lower(add(base + both, other))
    return lower(base + lax.psum(both, "tensor"))


def both_halves(half, axis=0):
    other = to_twin(half)
    first = lax.axis_index("pipe") % 2 == 0
    return jnp.concatenate(
        [jnp.where(first, half, other), jnp.where(first, other, half)], axis=axis
    )


def to_next_column(half):
    sections = lax.axis_size("pipe")
    return everywhere(half, lambda p, t, d: ((p + 2) % sections, t, d))


def first_states(chosen, parts):
    rank = lax.axis_index("dp")
    size = lax.axis_size("dp")
    window, width = chosen.shape
    share = width // size
    states = jnp.zeros((size, window, share), chosen.dtype)
    for flip, moves in enumerate((None, SWAP, SKIP, MIRROR)):
        piece = lax.dynamic_slice_in_dim(chosen, (rank ^ flip) * share, share, 1)
        if flip:
            piece = along_dp(piece, moves)
        states = lax.dynamic_update_slice_in_dim(states, piece[None], rank ^ flip, 0)
    length = window // parts
    return [
        states[:, p * length : (p + 1) * length].reshape(size * length, share)
        for p in range(parts)
    ]


def all_columns(halves, work=None):
    half = jnp.concatenate(halves, axis=0)
    rank = lax.axis_index("dp")
    size = lax.axis_size("dp")
    pieces, _ = slot(half, None, work)
    rows, share = half.shape
    whole = jnp.zeros((rows, size * share), half.dtype)
    for flip, piece in enumerate(pieces):
        whole = lax.dynamic_update_slice_in_dim(whole, piece, (rank ^ flip) * share, 1)
    streams = len(halves)
    whole = both_halves(whole.reshape(streams, rows // streams, size * share), 1)
    return whole.reshape(2 * rows, size * share)


def merged_stats(stats, combine):
    pipes, tensors, dps = (lax.axis_size(a) for a in AXES)
    for axis, size in enumerate((pipes, tensors, dps)):
        bit = 1
        while bit < size:
            flips = [bit if i == axis else 0 for i in range(3)]
            other = everywhere(stats, lambda *c, f=flips: tuple(i ^ j for i, j in zip(c, f)))
            stats = combine(stats, other)
            bit *= 2
    return stats


def combine_stats(first, second):
    top = jnp.maximum(first[0], second[0])
    total = first[1] * jnp.exp(first[0] - top) + second[1] * jnp.exp(second[0] - top)
    return jnp.stack([top, total, first[2] + second[2], first[3] + second[3]])


def local(
    inputs,
    layer_gain,
    up_weight,
    down_weight,
    final_gain,
    value_head,
    q_head,
    target_head,
    actions,
    rewards,
    done,
    order,
):
    sections = lax.axis_size("pipe")
    micro = inputs.shape[0]
    window = inputs.shape[1]
    width_model = inputs.shape[2]
    share = width_model // lax.axis_size("dp")
    w_up, w_down = up_weight[0], down_weight[0]
    gain = lax.dynamic_slice_in_dim(layer_gain[0], lax.axis_index("dp") * share, share, 0)

    columns_here = q_head.shape[1]
    offset = lax.axis_index(AXES) * columns_here
    size = lax.axis_size("dp")
    parts = 2
    count = micro * window * size
    factor = width_model ** (-0.5)

    def shuffled(values):
        return values.reshape(micro, size, parts, window // parts).swapaxes(1, 2).reshape(-1)

    def natural(values):
        shape = values.shape[:-1]
        split = values.reshape(shape + (micro, parts, size, window // parts))
        return split.swapaxes(-3, -2).reshape(shape + (count,))

    action = jnp.take(actions, order, axis=0).reshape(-1)
    reward = jnp.take(rewards, order, axis=0).reshape(-1).astype(jnp.float32)
    finished = jnp.take(done, order, axis=0).reshape(-1).astype(jnp.float32)
    hit = shuffled(action)[:, None] == offset + lax.broadcasted_iota(
        jnp.int32, (1, columns_here), 1
    )

    chosen = jnp.take(inputs, order, axis=0)
    begun = {0: first_states(chosen[0], parts)}
    weights = Weights(w_up, w_down, gain)
    sent = weights.swap(0, (3,))
    weights.swap(0, (2, 1, 0), sent)
    weights.swap(1, (0, 1, 2, 3), begun[0][0])
    selected = hit.astype(jnp.bfloat16)
    targets = {}
    cuts = 8
    features = width_model // cuts

    def target_work(index):
        def compute(need):
            rows = lax.slice_in_dim(target_head, index * features, (index + 1) * features, axis=0)
            picked = lax.dot_general(
                need, rows, (((1,), (1,)), ((), ())), preferred_element_type=jnp.float32
            )
            return lower(picked)

        def take(made):
            targets[index] = made

        return (lambda: selected, compute, take)

    quarters = 4
    score_columns = columns_here // quarters
    scores = {}

    def score_work(pair, index):
        def compute(need):
            some = lax.slice_in_dim(
                q_head, index * score_columns, (index + 1) * score_columns, axis=1
            )
            return jnp.dot(need, some, preferred_element_type=jnp.float32) * factor

        def take(made):
            scores[pair, index] = made

        return (lambda: flats[pair], compute, take)

    weights.keep(0, 0, (3,), weights.make(0, 0, (3,), (weights.got[0][3],)))
    work = {
        0: {
            2: [weights.work(0, 0, (2,))],
            3: [weights.work(0, 0, (1, 0))],
            4: [weights.work(1, 0, (0, 1))],
        },
        1: {
            1: [weights.work(1, 0, (2, 3))],
            2: [weights.work(0, 1, (3, 2))],
            3: [weights.work(0, 1, (1,))],
            4: [weights.work(0, 1, (0,))],
        },
        2: {1: [weights.work(1, 1, (0, 1))], 2: [weights.work(1, 1, (2, 3))]},
        3: {2: [target_work(0)], 3: [target_work(1)]},
        4: {2: [target_work(2)], 3: [target_work(3)]},
        5: {2: [target_work(4)], 3: [target_work(5)]},
        6: {2: [target_work(6)], 3: [target_work(7)]},
    }
    columns = sections // 2
    column = lax.axis_index("pipe") // 2
    pending = list(begun[0])
    finals = {}
    own = None
    holder = None
    slots = 4 * (micro - 1 + columns)

    flats = {}

    def score_at(place):
        if micro < 2:
            return None
        first = 2 * place
        return {
            1: [score_work(pair, first) for pair in range(micro - 1)],
            2: [score_work(pair, first + 1) for pair in range(micro - 1)],
        }

    def flatten(pair, rest):
        raw = all_columns([finals[pair, p] for p in range(parts)], rest)
        wide = raw.astype(jnp.float32)
        scale_row = lax.rsqrt(jnp.mean(wide * wide, axis=-1, keepdims=True) + EPS)
        flats[pair] = lower(wide * scale_row * final_gain)

    def head(pair):
        flat = flats[pair]
        rows = slice(pair * count // micro, (pair + 1) * count // micro)
        values = jnp.dot(flat, value_head, preferred_element_type=jnp.float32) * factor
        if (pair, 0) in scores:
            logits = jnp.concatenate([scores[pair, i] for i in range(quarters)], axis=1)
        else:
            logits = jnp.dot(flat, q_head, preferred_element_type=jnp.float32) * factor
        local_top = jnp.max(logits, axis=-1)
        local_total = jnp.sum(jnp.exp(logits - local_top[:, None]), axis=-1)
        taken_part = jnp.sum(jnp.where(hit[rows], logits, 0.0), axis=-1)
        target_part = 0.0
        for index in range(cuts):
            some = flat[:, index * features : (index + 1) * features].astype(jnp.float32)
            target_part = target_part + jnp.sum(
                some * targets[index][rows].astype(jnp.float32), axis=-1
            )
        stats = jnp.stack([local_top, local_total, taken_part, target_part * factor])
        return logits, values, stats

    for step in range(slots + 1):
        part, parity = step % 2, (step // 2) % 2
        reduction = None
        if step < slots:
            reduction = Reduction(pending[part], weights, parity)
        doing = score_at(0) if step == slots else work.get(step)
        pieces, fresh = slot(own, reduction, doing)
        if step == 1 and micro > 1:
            late, _ = lax.optimization_barrier((chosen, fresh))
            for m in range(1, micro):
                begun[m] = first_states(late[m], parts)
        if own is not None:
            total = lowered(pieces, weights, holder.parity)
            half = half_output(holder.states, total)
            before = step - 1
            if holder.parity == 0:
                pending[before % 2] = both_halves(half)
            else:
                moved = to_next_column(half)
                entering = before // 4 + 1
                leaving = before // 4 - (columns - 1)
                if step < slots - 1:
                    new = both_halves(moved)
                    if entering < micro:
                        new = jnp.where(column == 0, begun[entering][before % 2], new)
                    pending[before % 2] = new
                if leaving >= 0:
                    held = jnp.where(column == columns - 1, half, moved)
                    for turn in range(1, columns - 1):
                        moved = to_next_column(moved)
                        held = jnp.where(column == turn, moved, held)
                    finals[leaving, before % 2] = held
                    if before % 2 == parts - 1:
                        rest = score_at(1) if step == slots else None
                        flatten(leaving, rest)
        own, holder = fresh, reduction

    parts_of = [head(m) for m in range(micro)]
    stats = merged_stats(jnp.concatenate([p[2] for p in parts_of], axis=1), combine_stats)
    lse_rows = stats[0] + jnp.log(stats[1])
    flat = jnp.concatenate([flats[m] for m in range(micro)], axis=0)
    logits = jnp.concatenate([p[0] for p in parts_of], axis=0)
    probs = lower(jnp.exp(logits - lse_rows[:, None]))
    rows = natural(
        jnp.stack([jnp.concatenate([p[1] for p in parts_of]), lse_rows, stats[2], stats[3]])
    )
    values, lse, taken, target_taken = rows[0], rows[1], rows[2], rows[3]
    windows = values.reshape(-1, window)
    following = jnp.concatenate(
        [windows[:, 1:], jnp.zeros((windows.shape[0], 1), jnp.float32)], axis=1
    ).reshape(-1)
    bootstrap = 0.5 * reward + GAMMA * (1.0 - finished) * following
    td_value = taken - bootstrap
    advantage = target_taken - values
    weight = jnp.where(advantage < 0, 1.0 - TAU, TAU)
    value_loss = jnp.mean(weight * advantage * advantage)
    q_loss = jnp.mean(td_value * td_value + ALPHA * (lse - taken))
    scale = VQ * factor / count
    flat, probs = lax.optimization_barrier((flat, probs))
    gathered_sum = lax.dot_general(
        flat, probs, (((0,), (0,)), ((), ())), preferred_element_type=jnp.float32
    )
    lse_grad = (gathered_sum * scale).astype(jnp.bfloat16)
    shape = (micro, count // micro)
    return (
        values.reshape(shape),
        advantage.reshape(shape),
        td_value.reshape(shape),
        value_loss,
        q_loss,
        lse_grad,
    )


def solution(mesh):
    in_specs = (
        P(None, "dp", None),
        P("pipe", None),
        P("pipe", "dp", "tensor"),
        P("pipe", "tensor", "dp"),
        P(),
        P(),
        P(None, ("pipe", "tensor", "dp")),
        P(None, ("pipe", "tensor", "dp")),
        P(),
        P(),
        P(),
        P(),
    )
    out_specs = (P(), P(), P(), P(), P(), P(None, ("pipe", "tensor", "dp")))
    return jax.shard_map(local, mesh=mesh, in_specs=in_specs, out_specs=out_specs, check_vma=False)
```

```python
import jax
import jax.numpy as jnp
from jax import lax
from jax.sharding import PartitionSpec as P

VQ = 65536


EPS = 1e-05
GAMMA = 0.99
TAU = 0.7
ALPHA = 0.5

AXES = ("pipe", "tensor", "dp")


def send(block, pairs):
    _, tensors, dps = (lax.axis_size(a) for a in AXES)

    def flat(c):
        return (c[0] * tensors + c[1]) * dps + c[2]

    return lax.ppermute(block, AXES, [(flat(a), flat(b)) for a, b in pairs])


def everywhere(block, route):
    pipes, tensors, dps = (range(lax.axis_size(a)) for a in AXES)
    cells = [(p, t, d) for p in pipes for t in tensors for d in dps]
    return send(block, [(c, route(*c)) for c in cells])


def along_dp(block, moves):
    pipes, tensors = range(lax.axis_size("pipe")), range(lax.axis_size("tensor"))
    pairs = [((p, t, a), (p, t, b)) for p in pipes for t in tensors for a, b in moves]
    return send(block, pairs)


SWAP = ((0, 1), (1, 0), (2, 3), (3, 2))
SKIP = ((0, 2), (2, 0), (1, 3), (3, 1))
MIRROR = ((0, 3), (3, 0), (1, 2), (2, 1))


def across_middle(block):
    return everywhere(
        block, lambda p, t, d: (p, t, 3 - d) if d in (1, 2) else (p ^ 1, t, d)
    )


def to_twin(block):
    return everywhere(block, lambda p, t, d: (p ^ 1, t, d))


def lower(values):
    return values.astype(jnp.bfloat16)


def add(values, other):
    return values + other.astype(jnp.float32)


def only(where, values):
    return jnp.where(where, values.astype(jnp.float32), 0.0)


def is_inner():
    rank = lax.axis_index("dp")
    return (rank == 1) | (rank == 2)


class Weights:
    def __init__(self, w_up, w_down, gain):
        self.gain, self.gain_got = gain, to_twin(gain)
        self.core = lax.axis_index("pipe") % 2
        self.half = w_up.shape[1] // 2
        self.block = self.half // lax.axis_size("dp")
        self.mine = (w_up, w_down)
        self.got = ({}, {})
        self.ready = {}

    def swap(self, kind, flips, token=None):
        for flip in flips:
            sent = self.cut(kind, 1 - self.core, flip, token)
            self.got[kind][flip] = to_twin(sent)
        return sent

    def cut(self, kind, half, flip, token=None):
        rank = lax.axis_index("dp")
        if token is not None:
            rank, _ = lax.optimization_barrier((rank, token))
        first = half * self.half + (rank ^ flip) * self.block
        return lax.dynamic_slice_in_dim(self.mine[kind], first, self.block, 1 - kind)

    def section_gain(self, parity):
        return jnp.where(self.core == parity, self.gain, self.gain_got)

    def make(self, kind, flip, moved):
        kept = self.cut(kind, self.core, flip, moved)
        return tuple(jnp.where(self.core == parity, kept, moved) for parity in (0, 1))

    def keep(self, kind, flip, made):
        for parity in (0, 1):
            self.ready[kind, parity, flip] = made[parity]

    def work(self, kind, flip):
        return (
            lambda: self.got[kind][flip],
            lambda moved: self.make(kind, flip, moved),
            lambda made: self.keep(kind, flip, made),
        )

    def up_block(self, parity, flip):
        return self.ready[0, parity, flip]

    def down_block(self, parity, flip):
        return self.ready[1, parity, flip]


class Reduction:
    def __init__(self, states, weights, parity):
        width = states.shape[1]
        wide = states.astype(jnp.float32)
        self.states = states
        self.parity = parity
        scaled = lower(wide * weights.section_gain(parity))
        self.squares = jnp.sum(wide * wide, axis=1)
        self.width = width * lax.axis_size("dp")

        def part(flip):
            block = weights.up_block(parity, flip)
            return jnp.dot(scaled, block, preferred_element_type=jnp.float32)

        self.part = part
        self.part3 = part(3)


def together(moves, work=()):
    values = tuple(value for value, _ in moves)
    needs = tuple(need() for need, _, _ in work)
    values, needs = lax.optimization_barrier((values, needs))
    outs = tuple(move(value) for value, (_, move) in zip(values, moves))
    made = tuple(compute(need) for need, (_, compute, _) in zip(needs, work))
    outs, made = lax.optimization_barrier((outs, made))
    for result, (_, _, take) in zip(made, work):
        take(result)
    return outs


def swap_dp(block):
    return along_dp(block, SWAP)


def skip_dp(block):
    return along_dp(block, SKIP)


def slot(own, reduction, work=None):
    inner = is_inner()
    y = reduction
    pieces = None
    work = work or {}
    if own is not None:
        near1, middle1 = together(
            [(own, swap_dp), (own, across_middle)], work.get(1, ())
        )
    if own is None:
        got, other = together(
            [(lower(y.part3), swap_dp), (y.squares, swap_dp)], work.get(2, ())
        )
    elif y is None:
        got, middle2 = together(
            [(middle1, swap_dp), (near1, across_middle)], work.get(2, ())
        )
    else:
        swapped = jnp.where(inner, middle1, lower(y.part3))
        got, middle2, other = together(
            [(swapped, swap_dp), (near1, across_middle), (y.squares, swap_dp)], work.get(2, ())
        )
    if y is None:
        (got2,) = together([(middle2, swap_dp)], work.get(3, ()))
    else:
        squares = y.squares + other
        part2 = y.part(2)
        crossed = lower(add(part2, got))
        swapped = lower(part2) if own is None else jnp.where(inner, middle2, lower(part2))
        got2, middle3, other = together(
            [(swapped, swap_dp), (crossed, across_middle), (squares, skip_dp)], work.get(3, ())
        )
        factor = lax.rsqrt((squares + other) / y.width + EPS)[:, None]
    if own is not None:
        pieces = (own, near1, jnp.where(inner, middle2, got), jnp.where(inner, middle1, got2))
    if y is None:
        return pieces, None
    last, cross = together(
        [
            (lower(y.part(1) + only(inner, middle3)), swap_dp),
            (lower(add(y.part3, got2)), across_middle),
        ],
        work.get(4, ()),
    )
    upper = (add(y.part(0), last) + only(inner, cross)) * factor
    return pieces, lower(jax.nn.silu(upper))


def lowered(pieces, weights, parity):
    total = None
    for flip, piece in enumerate(pieces):
        block = weights.down_block(parity, flip)
        product = jnp.dot(piece, block, preferred_element_type=jnp.float32)
        total = product if total is None else total + product
    return total


def half_output(states, total):
    core = lax.axis_index("pipe") % 2
    half = states.shape[0] // 2

    def cut(values, index):
        return lax.dynamic_slice_in_dim(values, index * half, half, 0)

    both = add(cut(total, core), to_twin(lower(cut(total, 1 - core))))
    base = cut(states, core).astype(jnp.float32)
    if lax.axis_size("tensor") == 2:
        other = everywhere(lower(both), lambda p, t, d: (p, 1 - t, d))
        return lower(add(base + both, other))
    return lower(base + lax.psum(both, "tensor"))


def both_halves(half, axis=0):
    other = to_twin(half)
    first = lax.axis_index("pipe") % 2 == 0
    return jnp.concatenate(
        [jnp.where(first, half, other), jnp.where(first, other, half)], axis=axis
    )


def to_next_column(half):
    sections = lax.axis_size("pipe")
    return everywhere(half, lambda p, t, d: ((p + 2) % sections, t, d))


def first_states(chosen, parts):
    rank = lax.axis_index("dp")
    size = lax.axis_size("dp")
    window, width = chosen.shape
    share = width // size
    states = jnp.zeros((size, window, share), chosen.dtype)
    for flip, moves in enumerate((None, SWAP, SKIP, MIRROR)):
        piece = lax.dynamic_slice_in_dim(chosen, (rank ^ flip) * share, share, 1)
        if flip:
            piece = along_dp(piece, moves)
        states = lax.dynamic_update_slice_in_dim(states, piece[None], rank ^ flip, 0)
    length = window // parts
    return [
        states[:, p * length : (p + 1) * length].reshape(size * length, share)
        for p in range(parts)
    ]


def all_columns(halves, work=None):
    half = jnp.concatenate(halves, axis=0)
    rank = lax.axis_index("dp")
    size = lax.axis_size("dp")
    pieces, _ = slot(half, None, work)
    rows, share = half.shape
    whole = jnp.zeros((rows, size * share), half.dtype)
    for flip, piece in enumerate(pieces):
        whole = lax.dynamic_update_slice_in_dim(whole, piece, (rank ^ flip) * share, 1)
    streams = len(halves)
    whole = both_halves(whole.reshape(streams, rows // streams, size * share), 1)
    return whole.reshape(2 * rows, size * share)


def merged_stats(stats, combine):
    pipes, tensors, dps = (lax.axis_size(a) for a in AXES)

    def met(value, flips):
        others = [
            everywhere(value, lambda *c, f=f: tuple(i ^ j for i, j in zip(c, f))) for f in flips
        ]
        for other in others:
            value = combine(value, other)
        return value

    if tensors == 2:
        stats = met(stats, [(1, 0, 0), (0, 1, 0), (1, 1, 0)])
    else:
        stats = met(stats, [(1, 0, 0)])
        bit = 1
        while bit < tensors:
            stats = met(stats, [(0, bit, 0)])
            bit *= 2
    bit = 2
    while bit < pipes:
        stats = met(stats, [(bit, 0, 0)])
        bit *= 2
    return met(stats, [(0, 0, turn) for turn in range(1, dps)])


def combine_stats(first, second):
    top = jnp.maximum(first[0], second[0])
    total = first[1] * jnp.exp(first[0] - top) + second[1] * jnp.exp(second[0] - top)
    return jnp.stack([top, total, first[2] + second[2], first[3] + second[3]])


def local(
    inputs,
    layer_gain,
    up_weight,
    down_weight,
    final_gain,
    value_head,
    q_head,
    target_head,
    actions,
    rewards,
    done,
    order,
):
    sections = lax.axis_size("pipe")
    micro = inputs.shape[0]
    window = inputs.shape[1]
    width_model = inputs.shape[2]
    share = width_model // lax.axis_size("dp")
    w_up, w_down = up_weight[0], down_weight[0]
    gain = lax.dynamic_slice_in_dim(layer_gain[0], lax.axis_index("dp") * share, share, 0)

    columns_here = q_head.shape[1]
    offset = lax.axis_index(AXES) * columns_here
    size = lax.axis_size("dp")
    parts = 2
    count = micro * window * size
    factor = width_model ** (-0.5)

    def shuffled(values):
        return values.reshape(micro, size, parts, window // parts).swapaxes(1, 2).reshape(-1)

    def natural(values):
        shape = values.shape[:-1]
        split = values.reshape(shape + (micro, parts, size, window // parts))
        return split.swapaxes(-3, -2).reshape(shape + (count,))

    action = jnp.take(actions, order, axis=0).reshape(-1)
    reward = jnp.take(rewards, order, axis=0).reshape(-1).astype(jnp.float32)
    finished = jnp.take(done, order, axis=0).reshape(-1).astype(jnp.float32)
    hit = shuffled(action)[:, None] == offset + lax.broadcasted_iota(
        jnp.int32, (1, columns_here), 1
    )

    chosen = jnp.take(inputs, order, axis=0)
    begun = {0: first_states(chosen[0], parts)}
    weights = Weights(w_up, w_down, gain)
    sent = weights.swap(0, (3,))
    weights.swap(0, (2, 1, 0), sent)
    weights.swap(1, (0, 1, 2, 3), begun[0][0])
    selected = hit.astype(jnp.bfloat16)
    targets = {}
    cuts = 8
    features = width_model // cuts

    def target_work(index):
        def compute(need):
            rows = lax.slice_in_dim(target_head, index * features, (index + 1) * features, axis=0)
            picked = lax.dot_general(
                need, rows, (((1,), (1,)), ((), ())), preferred_element_type=jnp.float32
            )
            return lower(picked)

        def take(made):
            targets[index] = made

        return (lambda: selected, compute, take)

    quarters = 4
    score_columns = columns_here // quarters
    scores = {}

    def score_work(pair, index):
        def compute(need):
            some = lax.slice_in_dim(
                q_head, index * score_columns, (index + 1) * score_columns, axis=1
            )
            return jnp.dot(need, some, preferred_element_type=jnp.float32) * factor

        def take(made):
            scores[pair, index] = made

        return (lambda: flats[pair], compute, take)

    weights.keep(0, 3, lax.optimization_barrier(weights.make(0, 3, weights.got[0][3])))
    pick = weights.work
    work = {
        0: {2: [pick(0, 2)], 3: [pick(0, 1)], 4: [pick(0, 0), pick(1, 0)]},
        1: {1: [pick(1, 1)], 2: [pick(1, 2)], 3: [pick(1, 3)]},
    }
    for index in range(cuts):
        work.setdefault(2 + index // 2, {})[2 + index % 2] = [target_work(index)]
    columns = sections // 2
    column = lax.axis_index("pipe") // 2
    pending = list(begun[0])
    finals = {}
    own = None
    holder = None
    slots = 4 * (micro - 1 + columns)

    flats = {}

    def score_at(place):
        if micro < 2:
            return None
        first = 2 * place
        return {
            1: [score_work(pair, first) for pair in range(micro - 1)],
            2: [score_work(pair, first + 1) for pair in range(micro - 1)],
        }

    def flatten(pair, rest):
        raw = all_columns([finals[pair, p] for p in range(parts)], rest)
        wide = raw.astype(jnp.float32)
        scale_row = lax.rsqrt(jnp.mean(wide * wide, axis=-1, keepdims=True) + EPS)
        flats[pair] = lower(wide * scale_row * final_gain)

    def head(pair):
        flat = flats[pair]
        rows = slice(pair * count // micro, (pair + 1) * count // micro)
        values = jnp.dot(flat, value_head, preferred_element_type=jnp.float32) * factor
        if (pair, 0) in scores:
            logits = jnp.concatenate([scores[pair, i] for i in range(quarters)], axis=1)
        else:
            logits = jnp.dot(flat, q_head, preferred_element_type=jnp.float32) * factor
        local_top = jnp.max(logits, axis=-1)
        local_total = jnp.sum(jnp.exp(logits - local_top[:, None]), axis=-1)
        taken_part = jnp.sum(jnp.where(hit[rows], logits, 0.0), axis=-1)
        target_part = 0.0
        for index in range(cuts):
            some = flat[:, index * features : (index + 1) * features].astype(jnp.float32)
            target_part = target_part + jnp.sum(
                some * targets[index][rows].astype(jnp.float32), axis=-1
            )
        stats = jnp.stack([local_top, local_total, taken_part, target_part * factor])
        return logits, values, stats

    for step in range(slots + 1):
        part, parity = step % 2, (step // 2) % 2
        reduction = None
        if step < slots:
            reduction = Reduction(pending[part], weights, parity)
        doing = score_at(0) if step == slots else work.get(step)
        pieces, fresh = slot(own, reduction, doing)
        if step == 1 and micro > 1:
            late, _ = lax.optimization_barrier((chosen, fresh))
            for m in range(1, micro):
                begun[m] = first_states(late[m], parts)
        if own is not None:
            total = lowered(pieces, weights, holder.parity)
            half = half_output(holder.states, total)
            before = step - 1
            if holder.parity == 0:
                pending[before % 2] = both_halves(half)
            else:
                moved = to_next_column(half)
                entering = before // 4 + 1
                leaving = before // 4 - (columns - 1)
                if step < slots - 1:
                    new = both_halves(moved)
                    if entering < micro:
                        new = jnp.where(column == 0, begun[entering][before % 2], new)
                    pending[before % 2] = new
                if leaving >= 0:
                    held = jnp.where(column == columns - 1, half, moved)
                    for turn in range(1, columns - 1):
                        moved = to_next_column(moved)
                        held = jnp.where(column == turn, moved, held)
                    finals[leaving, before % 2] = held
                    if before % 2 == parts - 1:
                        rest = score_at(1) if step == slots else None
                        flatten(leaving, rest)
        own, holder = fresh, reduction

    parts_of = [head(m) for m in range(micro)]
    stats = merged_stats(jnp.concatenate([p[2] for p in parts_of], axis=1), combine_stats)
    lse_rows = stats[0] + jnp.log(stats[1])
    flat = jnp.concatenate([flats[m] for m in range(micro)], axis=0)
    logits = jnp.concatenate([p[0] for p in parts_of], axis=0)
    probs = lower(jnp.exp(logits - lse_rows[:, None]))
    rows = natural(
        jnp.stack([jnp.concatenate([p[1] for p in parts_of]), lse_rows, stats[2], stats[3]])
    )
    values, lse, taken, target_taken = rows[0], rows[1], rows[2], rows[3]
    windows = values.reshape(-1, window)
    following = jnp.concatenate(
        [windows[:, 1:], jnp.zeros((windows.shape[0], 1), jnp.float32)], axis=1
    ).reshape(-1)
    bootstrap = 0.5 * reward + GAMMA * (1.0 - finished) * following
    td_value = taken - bootstrap
    advantage = target_taken - values
    weight = jnp.where(advantage < 0, 1.0 - TAU, TAU)
    value_loss = jnp.mean(weight * advantage * advantage)
    q_loss = jnp.mean(td_value * td_value + ALPHA * (lse - taken))
    scale = VQ * factor / count
    flat, probs = lax.optimization_barrier((flat, probs))
    gathered_sum = lax.dot_general(
        flat, probs, (((0,), (0,)), ((), ())), preferred_element_type=jnp.float32
    )
    lse_grad = (gathered_sum * scale).astype(jnp.bfloat16)
    shape = (micro, count // micro)
    return (
        values.reshape(shape),
        advantage.reshape(shape),
        td_value.reshape(shape),
        value_loss,
        q_loss,
        lse_grad,
    )


def solution(mesh):
    in_specs = (
        P(None, "dp", None),
        P("pipe", None),
        P("pipe", "dp", "tensor"),
        P("pipe", "tensor", "dp"),
        P(),
        P(),
        P(None, ("pipe", "tensor", "dp")),
        P(None, ("pipe", "tensor", "dp")),
        P(),
        P(),
        P(),
        P(),
    )
    out_specs = (P(), P(), P(), P(), P(), P(None, ("pipe", "tensor", "dp")))
    return jax.shard_map(local, mesh=mesh, in_specs=in_specs, out_specs=out_specs, check_vma=False)
```

```python
import jax
import jax.numpy as jnp
from jax import lax
from jax.sharding import PartitionSpec as P

VQ = 65536


EPS = 1e-05
GAMMA = 0.99
TAU = 0.7
ALPHA = 0.5

AXES = ("pipe", "tensor", "dp")


def send(block, pairs):
    _, tensors, dps = (lax.axis_size(a) for a in AXES)

    def flat(c):
        return (c[0] * tensors + c[1]) * dps + c[2]

    return lax.ppermute(block, AXES, [(flat(a), flat(b)) for a, b in pairs])


def everywhere(block, route):
    pipes, tensors, dps = (range(lax.axis_size(a)) for a in AXES)
    cells = [(p, t, d) for p in pipes for t in tensors for d in dps]
    return send(block, [(c, route(*c)) for c in cells])


def along_dp(block, moves):
    pipes, tensors = range(lax.axis_size("pipe")), range(lax.axis_size("tensor"))
    pairs = [((p, t, a), (p, t, b)) for p in pipes for t in tensors for a, b in moves]
    return send(block, pairs)


SWAP = ((0, 1), (1, 0), (2, 3), (3, 2))
SKIP = ((0, 2), (2, 0), (1, 3), (3, 1))
MIRROR = ((0, 3), (3, 0), (1, 2), (2, 1))


def across_middle(block):
    return everywhere(
        block, lambda p, t, d: (p, t, 3 - d) if d in (1, 2) else (p ^ 1, t, d)
    )


def to_twin(block):
    return everywhere(block, lambda p, t, d: (p ^ 1, t, d))


def lower(values):
    return values.astype(jnp.bfloat16)


def add(values, other):
    return values + other.astype(jnp.float32)


def only(where, values):
    return jnp.where(where, values.astype(jnp.float32), 0.0)


def is_inner():
    rank = lax.axis_index("dp")
    return (rank == 1) | (rank == 2)


class Weights:
    def __init__(self, w_up, w_down, gain):
        self.gain, self.gain_got = gain, to_twin(gain)
        self.core = lax.axis_index("pipe") % 2
        self.half = w_up.shape[1] // 2
        self.block = self.half // lax.axis_size("dp")
        self.mine = (w_up, w_down)
        self.got = ({}, {})
        self.ready = {}

    def swap(self, kind, flips, token=None):
        for flip in flips:
            sent = self.cut(kind, 1 - self.core, flip, token)
            self.got[kind][flip] = to_twin(sent)
        return sent

    def cut(self, kind, half, flip, token=None):
        rank = lax.axis_index("dp")
        if token is not None:
            rank, _ = lax.optimization_barrier((rank, token))
        first = half * self.half + (rank ^ flip) * self.block
        return lax.dynamic_slice_in_dim(self.mine[kind], first, self.block, 1 - kind)

    def section_gain(self, parity):
        return jnp.where(self.core == parity, self.gain, self.gain_got)

    def make(self, kind, flip, moved):
        kept = self.cut(kind, self.core, flip, moved)
        return tuple(jnp.where(self.core == parity, kept, moved) for parity in (0, 1))

    def keep(self, kind, flip, made):
        for parity in (0, 1):
            self.ready[kind, parity, flip] = made[parity]

    def work(self, kind, flip):
        return (
            lambda: self.got[kind][flip],
            lambda moved: self.make(kind, flip, moved),
            lambda made: self.keep(kind, flip, made),
        )

    def up_block(self, parity, flip):
        return self.ready[0, parity, flip]

    def down_block(self, parity, flip):
        return self.ready[1, parity, flip]


class Reduction:
    def __init__(self, states, weights, parity):
        width = states.shape[1]
        wide = states.astype(jnp.float32)
        self.states = states
        self.parity = parity
        scaled = lower(wide * weights.section_gain(parity))
        self.squares = jnp.sum(wide * wide, axis=1)
        self.width = width * lax.axis_size("dp")

        def part(flip):
            block = weights.up_block(parity, flip)
            return jnp.dot(scaled, block, preferred_element_type=jnp.float32)

        self.part = part
        self.part3 = part(3)


def together(moves, work=()):
    values = tuple(value for value, _ in moves)
    needs = tuple(need() for need, _, _ in work)
    values, needs = lax.optimization_barrier((values, needs))
    outs = tuple(move(value) for value, (_, move) in zip(values, moves))
    made = tuple(compute(need) for need, (_, compute, _) in zip(needs, work))
    outs, made = lax.optimization_barrier((outs, made))
    for result, (_, _, take) in zip(made, work):
        take(result)
    return outs


def swap_dp(block):
    return along_dp(block, SWAP)


def skip_dp(block):
    return along_dp(block, SKIP)


def slot(own, reduction, work=None):
    inner = is_inner()
    y = reduction
    pieces = None
    work = work or {}
    if own is not None:
        near1, middle1 = together(
            [(own, swap_dp), (own, across_middle)], work.get(1, ())
        )
    if own is None:
        got, other = together(
            [(lower(y.part3), swap_dp), (y.squares, swap_dp)], work.get(2, ())
        )
    elif y is None:
        got, middle2 = together(
            [(middle1, swap_dp), (near1, across_middle)], work.get(2, ())
        )
    else:
        swapped = jnp.where(inner, middle1, lower(y.part3))
        got, middle2, other = together(
            [(swapped, swap_dp), (near1, across_middle), (y.squares, swap_dp)], work.get(2, ())
        )
    if y is None:
        (got2,) = together([(middle2, swap_dp)], work.get(3, ()))
    else:
        squares = y.squares + other
        part2 = y.part(2)
        crossed = lower(add(part2, got))
        swapped = lower(part2) if own is None else jnp.where(inner, middle2, lower(part2))
        got2, middle3, other = together(
            [(swapped, swap_dp), (crossed, across_middle), (squares, skip_dp)], work.get(3, ())
        )
        factor = lax.rsqrt((squares + other) / y.width + EPS)[:, None]
    if own is not None:
        pieces = (own, near1, jnp.where(inner, middle2, got), jnp.where(inner, middle1, got2))
    if y is None:
        return pieces, None
    last, cross = together(
        [
            (lower(y.part(1) + only(inner, middle3)), swap_dp),
            (lower(add(y.part3, got2)), across_middle),
        ],
        work.get(4, ()),
    )
    upper = (add(y.part(0), last) + only(inner, cross)) * factor
    return pieces, lower(jax.nn.silu(upper))


def lowered(pieces, weights, parity):
    total = None
    for flip, piece in enumerate(pieces):
        block = weights.down_block(parity, flip)
        product = jnp.dot(piece, block, preferred_element_type=jnp.float32)
        total = product if total is None else total + product
    return total


def half_output(states, total):
    core = lax.axis_index("pipe") % 2
    half = states.shape[0] // 2

    def cut(values, index):
        return lax.dynamic_slice_in_dim(values, index * half, half, 0)

    both = add(cut(total, core), to_twin(lower(cut(total, 1 - core))))
    base = cut(states, core).astype(jnp.float32)
    if lax.axis_size("tensor") == 2:
        other = everywhere(lower(both), lambda p, t, d: (p, 1 - t, d))
        return lower(add(base + both, other))
    return lower(base + lax.psum(both, "tensor"))


def both_halves(half, axis=0):
    other = to_twin(half)
    first = lax.axis_index("pipe") % 2 == 0
    return jnp.concatenate(
        [jnp.where(first, half, other), jnp.where(first, other, half)], axis=axis
    )


def to_next_column(half):
    sections = lax.axis_size("pipe")
    return everywhere(half, lambda p, t, d: ((p + 2) % sections, t, d))


def first_states(chosen, parts):
    rank = lax.axis_index("dp")
    size = lax.axis_size("dp")
    window, width = chosen.shape
    share = width // size
    states = jnp.zeros((size, window, share), chosen.dtype)
    for flip, moves in enumerate((None, SWAP, SKIP, MIRROR)):
        piece = lax.dynamic_slice_in_dim(chosen, (rank ^ flip) * share, share, 1)
        if flip:
            piece = along_dp(piece, moves)
        states = lax.dynamic_update_slice_in_dim(states, piece[None], rank ^ flip, 0)
    length = window // parts
    return [
        states[:, p * length : (p + 1) * length].reshape(size * length, share)
        for p in range(parts)
    ]


def all_columns(halves, work=None):
    half = jnp.concatenate(halves, axis=0)
    rank = lax.axis_index("dp")
    size = lax.axis_size("dp")
    pieces, _ = slot(half, None, work)
    rows, share = half.shape
    whole = jnp.zeros((rows, size * share), half.dtype)
    for flip, piece in enumerate(pieces):
        whole = lax.dynamic_update_slice_in_dim(whole, piece, (rank ^ flip) * share, 1)
    streams = len(halves)
    whole = both_halves(whole.reshape(streams, rows // streams, size * share), 1)
    return whole.reshape(2 * rows, size * share)


def merged_stats(stats, combine):
    pipes, tensors, dps = (lax.axis_size(a) for a in AXES)

    def met(value, flips):
        others = [
            everywhere(value, lambda *c, f=f: tuple(i ^ j for i, j in zip(c, f))) for f in flips
        ]
        for other in others:
            value = combine(value, other)
        return value

    if tensors == 2:
        stats = met(stats, [(1, 0, 0), (0, 1, 0), (1, 1, 0)])
    else:
        stats = met(stats, [(1, 0, 0)])
        bit = 1
        while bit < tensors:
            stats = met(stats, [(0, bit, 0)])
            bit *= 2
    bit = 2
    while bit < pipes:
        stats = met(stats, [(bit, 0, 0)])
        bit *= 2
    return met(stats, [(0, 0, turn) for turn in range(1, dps)])


def combine_stats(first, second):
    top = jnp.maximum(first[0], second[0])
    total = first[1] * jnp.exp(first[0] - top) + second[1] * jnp.exp(second[0] - top)
    return jnp.stack([top, total, first[2] + second[2], first[3] + second[3]])


def local(
    inputs,
    layer_gain,
    up_weight,
    down_weight,
    final_gain,
    value_head,
    q_head,
    target_head,
    actions,
    rewards,
    done,
    order,
):
    sections = lax.axis_size("pipe")
    micro = inputs.shape[0]
    window = inputs.shape[1]
    width_model = inputs.shape[2]
    share = width_model // lax.axis_size("dp")
    w_up, w_down = up_weight[0], down_weight[0]
    gain = lax.dynamic_slice_in_dim(layer_gain[0], lax.axis_index("dp") * share, share, 0)

    columns_here = q_head.shape[1]
    offset = lax.axis_index(AXES) * columns_here
    size = lax.axis_size("dp")
    parts = 2
    count = micro * window * size
    factor = width_model ** (-0.5)

    def shuffled(values):
        return values.reshape(micro, size, parts, window // parts).swapaxes(1, 2).reshape(-1)

    def natural(values):
        shape = values.shape[:-1]
        split = values.reshape(shape + (micro, parts, size, window // parts))
        return split.swapaxes(-3, -2).reshape(shape + (count,))

    action = jnp.take(actions, order, axis=0).reshape(-1)
    reward = jnp.take(rewards, order, axis=0).reshape(-1).astype(jnp.float32)
    finished = jnp.take(done, order, axis=0).reshape(-1).astype(jnp.float32)
    hit = shuffled(action)[:, None] == offset + lax.broadcasted_iota(
        jnp.int32, (1, columns_here), 1
    )

    chosen = jnp.take(inputs, order, axis=0)
    begun = {0: first_states(chosen[0], parts)}
    weights = Weights(w_up, w_down, gain)
    sent = weights.swap(0, (3,))
    weights.swap(0, (2, 1, 0), sent)
    weights.swap(1, (0, 1, 2, 3), begun[0][0])
    selected = hit.astype(jnp.bfloat16)
    targets = {}
    cuts = 8
    features = width_model // cuts

    def target_work(index):
        def compute(need):
            rows = lax.slice_in_dim(target_head, index * features, (index + 1) * features, axis=0)
            picked = lax.dot_general(
                need, rows, (((1,), (1,)), ((), ())), preferred_element_type=jnp.float32
            )
            return lower(picked)

        def take(made):
            targets[index] = made

        return (lambda: selected, compute, take)

    quarters = 4
    score_columns = columns_here // quarters
    scores = {}

    def score_work(pair, index):
        def compute(need):
            some = lax.slice_in_dim(
                q_head, index * score_columns, (index + 1) * score_columns, axis=1
            )
            return jnp.dot(need, some, preferred_element_type=jnp.float32) * factor

        def take(made):
            scores[pair, index] = made

        return (lambda: flats[pair], compute, take)

    weights.keep(0, 3, lax.optimization_barrier(weights.make(0, 3, weights.got[0][3])))
    pick = weights.work
    work = {
        0: {2: [pick(0, 2)], 3: [pick(0, 1)], 4: [pick(0, 0), pick(1, 0)]},
        1: {1: [pick(1, 1)], 2: [pick(1, 2)], 3: [pick(1, 3)]},
    }
    for index in range(cuts):
        work.setdefault(2 + index // 2, {})[2 + index % 2] = [target_work(index)]
    columns = sections // 2
    column = lax.axis_index("pipe") // 2
    pending = list(begun[0])
    finals = {}
    own = None
    holder = None
    slots = 4 * (micro - 1 + columns)

    flats = {}

    def score_at(place):
        if micro < 2:
            return None
        first = 2 * place
        return {
            1: [score_work(pair, first) for pair in range(micro - 1)],
            2: [score_work(pair, first + 1) for pair in range(micro - 1)],
        }

    def flatten(pair, rest):
        raw = all_columns([finals[pair, p] for p in range(parts)], rest)
        wide = raw.astype(jnp.float32)
        scale_row = lax.rsqrt(jnp.mean(wide * wide, axis=-1, keepdims=True) + EPS)
        flats[pair] = lower(wide * scale_row * final_gain)

    def head(pair):
        flat = flats[pair]
        rows = slice(pair * count // micro, (pair + 1) * count // micro)
        values = jnp.dot(flat, value_head, preferred_element_type=jnp.float32) * factor
        if (pair, 0) in scores:
            logits = jnp.concatenate([scores[pair, i] for i in range(quarters)], axis=1)
        else:
            logits = jnp.dot(flat, q_head, preferred_element_type=jnp.float32) * factor
        local_top = jnp.max(logits, axis=-1)
        local_total = jnp.sum(jnp.exp(logits - local_top[:, None]), axis=-1)
        taken_part = jnp.sum(jnp.where(hit[rows], logits, 0.0), axis=-1)
        target_part = 0.0
        for index in range(cuts):
            some = flat[:, index * features : (index + 1) * features].astype(jnp.float32)
            target_part = target_part + jnp.sum(
                some * targets[index][rows].astype(jnp.float32), axis=-1
            )
        stats = jnp.stack([local_top, local_total, taken_part, target_part * factor])
        return logits, values, stats

    for step in range(slots + 1):
        part, parity = step % 2, (step // 2) % 2
        reduction = None
        if step < slots:
            reduction = Reduction(pending[part], weights, parity)
        doing = score_at(0) if step == slots else work.get(step)
        pieces, fresh = slot(own, reduction, doing)
        if step == 1 and micro > 1:
            late = chosen
            for m in range(1, micro):
                begun[m] = first_states(late[m], parts)
        if own is not None:
            total = lowered(pieces, weights, holder.parity)
            half = half_output(holder.states, total)
            before = step - 1
            if holder.parity == 0:
                pending[before % 2] = both_halves(half)
            else:
                moved = to_next_column(half)
                entering = before // 4 + 1
                leaving = before // 4 - (columns - 1)
                if step < slots - 1:
                    new = both_halves(moved)
                    if entering < micro:
                        new = jnp.where(column == 0, begun[entering][before % 2], new)
                    pending[before % 2] = new
                if leaving >= 0:
                    held = jnp.where(column == columns - 1, half, moved)
                    for turn in range(1, columns - 1):
                        moved = to_next_column(moved)
                        held = jnp.where(column == turn, moved, held)
                    finals[leaving, before % 2] = held
                    if before % 2 == parts - 1:
                        rest = score_at(1) if step == slots else None
                        flatten(leaving, rest)
        own, holder = fresh, reduction

    parts_of = [head(m) for m in range(micro)]
    stats = merged_stats(jnp.concatenate([p[2] for p in parts_of], axis=1), combine_stats)
    lse_rows = stats[0] + jnp.log(stats[1])
    flat = jnp.concatenate([flats[m] for m in range(micro)], axis=0)
    logits = jnp.concatenate([p[0] for p in parts_of], axis=0)
    probs = lower(jnp.exp(logits - lse_rows[:, None]))
    rows = natural(
        jnp.stack([jnp.concatenate([p[1] for p in parts_of]), lse_rows, stats[2], stats[3]])
    )
    values, lse, taken, target_taken = rows[0], rows[1], rows[2], rows[3]
    windows = values.reshape(-1, window)
    following = jnp.concatenate(
        [windows[:, 1:], jnp.zeros((windows.shape[0], 1), jnp.float32)], axis=1
    ).reshape(-1)
    bootstrap = 0.5 * reward + GAMMA * (1.0 - finished) * following
    td_value = taken - bootstrap
    advantage = target_taken - values
    weight = jnp.where(advantage < 0, 1.0 - TAU, TAU)
    value_loss = jnp.mean(weight * advantage * advantage)
    q_loss = jnp.mean(td_value * td_value + ALPHA * (lse - taken))
    scale = VQ * factor / count
    turned = lax.optimization_barrier(flat.T)
    turned, probs = lax.optimization_barrier((turned, probs))
    gathered_sum = jnp.dot(turned, probs, preferred_element_type=jnp.float32)
    lse_grad = (gathered_sum * scale).astype(jnp.bfloat16)
    shape = (micro, count // micro)
    return (
        values.reshape(shape),
        advantage.reshape(shape),
        td_value.reshape(shape),
        value_loss,
        q_loss,
        lse_grad,
    )


def solution(mesh):
    in_specs = (
        P(None, "dp", None),
        P("pipe", None),
        P("pipe", "dp", "tensor"),
        P("pipe", "tensor", "dp"),
        P(),
        P(),
        P(None, ("pipe", "tensor", "dp")),
        P(None, ("pipe", "tensor", "dp")),
        P(),
        P(),
        P(),
        P(),
    )
    out_specs = (P(), P(), P(), P(), P(), P(None, ("pipe", "tensor", "dp")))
    return jax.shard_map(local, mesh=mesh, in_specs=in_specs, out_specs=out_specs, check_vma=False)
```
